32 devices in a mesh: groups: 2 (over x), ctx: 8 (over z, y), head: 2 (over core).
Axes of the slice: x: 2, y: 2, z: 4, core: 2. Of those that a mesh axis runs over, the one named last changes fastest.
Arguments:
- queries: bfloat16 [2, 256, 64, 128], P('groups', 'ctx', 'head'), parts along dimension 0, may hold values from -400 to 400
- new_keys: bfloat16 [2, 256, 8, 128], P('groups', 'ctx', 'head'), parts along dimension 0, may hold values from -5 to 5
- new_values: bfloat16 [2, 256, 8, 128], P('groups', 'ctx', 'head'), parts along dimension 0, may hold values from -6 to 6
- history_keys: bfloat16 [2, 8192, 8, 128], P('groups', 'ctx', 'head'), parts along dimension 0, may hold values from -6 to 6
- history_values: bfloat16 [2, 8192, 8, 128], P('groups', 'ctx', 'head'), parts along dimension 0, may hold values from -6 to 6
- block_mask: int32 [2, 2, 64], P('groups', None, 'ctx'), parts along dimension 0, may hold values from 0 to 1, as said below
Outputs:
- attended: bfloat16 [2, 256, 64, 128], P('groups', 'ctx', 'head'), parts along dimension 0
The draws below stay inside these ranges and needn't reach their ends.
There are 2 independent parts, one for each index of `groups`. The reference program is written for one: setup_inputs(seed, part) draws one part's arguments, and reference() takes and returns one part's arrays. A program takes and returns all parts, laid end to end along the dimension named above; each array names one. Nothing has to cross between parts.
Inputs may be any that keep to these rules, and one draw needn't show every extreme that they name: `block_mask`: 0 or 1 for each pair of a block of 128 new tokens and a block of 128 history positions of the same session.
All inputs are finite; a program needn't handle non-finite values.
Results may differ from the reference program's by a relative error of at most 0.0013.
Values may be sent and summed in bfloat16 or wider, within the bound.
A program may use at most 64 MiB of HBM per device.

```python
import math
import jax
import jax.numpy as jnp
from jax import lax

QH = 64
KVH = 8
HD = 128
BLK = 128
SESS = 1
NEW = 256
CTX = 8192
QB = 2
HB = 64
HB_DEV = 8


def drawn_pair(key):
    base = jax.random.fold_in(key, 11)
    first_key, second_key = jax.random.split(base)
    keys_new = jnp.clip(jax.random.normal(first_key, (SESS, NEW, KVH, HD), jnp.float32), -5.0, 5.0)
    query_rows = jnp.clip(jax.random.normal(second_key, (SESS, NEW, QH, HD), jnp.float32), -5.0, 5.0)
    return (query_rows, keys_new)


def draw_queries(key, part):
    return drawn_pair(key)[0].astype(jnp.bfloat16)


def draw_new_keys(key, part):
    return drawn_pair(key)[1].astype(jnp.bfloat16)


def draw_block_mask(key, part):
    level_key, bits_key, row_key, col_key = jax.random.split(jax.random.fold_in(key, 23), 4)
    owners = HB // HB_DEV
    level = jax.random.randint(level_key, (SESS, 1, owners), 1, 4)
    level_full = jnp.repeat(level, HB_DEV, axis=2)
    bits = jax.random.randint(bits_key, (SESS, QB, HB), 0, 16)
    live = bits < level_full
    pick_row = jax.random.randint(row_key, (SESS, owners), 0, QB)
    pick_col = jax.random.randint(col_key, (SESS, owners), 0, HB_DEV)
    row_full = jnp.repeat(pick_row, HB_DEV, axis=1)[:, None, :]
    col_full = jnp.repeat(pick_col, HB_DEV, axis=1)[:, None, :]
    blocks = jnp.arange(HB)[None, None, :]
    rows = jnp.arange(QB)[None, :, None]
    forced = (rows == row_full) & (blocks % HB_DEV == col_full)
    return (live | forced).astype(jnp.int32)


def level_of(stream_key, shape, shards, smallest, top_value):
    def one(dim, blocks):
        draws = jax.random.uniform(jax.random.fold_in(jax.random.fold_in(stream_key, 6), dim), (blocks,), jnp.float32, smallest / len(shards), top_value / len(shards))
        return jnp.repeat(jnp.exp(draws), shape[dim] // blocks).reshape((-1,) + (1,) * (len(shape) - dim - 1))

    loudness = one(*shards[0])
    for cut in shards[1:]:
        loudness = loudness * one(*cut)
    return loudness


def gaussian(key, extent, spread, bound, cuts=(), held_as=jnp.bfloat16):
    entries = jax.random.normal(key, extent, jnp.float32) * spread
    if len(cuts) > 0:
        entries = level_of(key, extent, cuts, -0.22, 0.18) * entries
    return jnp.clip(entries, min=-bound, max=bound).astype(held_as)


def setup_inputs(seed: int = 0, part: int = 0) -> dict:
    keys = jax.random.split(jax.random.key(seed), 7)
    own_keys = jax.random.split(jax.random.fold_in(keys[6], part), 7)
    queries = draw_queries(jax.random.fold_in(jax.random.fold_in(keys[6], part), 71), part)
    new_keys = draw_new_keys(jax.random.fold_in(jax.random.fold_in(keys[6], part), 71), part)
    new_values = gaussian(own_keys[2], (SESS, NEW, KVH, HD), 1.0, 6.0, ((1, 8), (2, 2)))
    history_keys = gaussian(own_keys[3], (SESS, CTX, KVH, HD), 1.0, 6.0, ((1, 8), (2, 2)))
    history_values = gaussian(own_keys[4], (SESS, CTX, KVH, HD), 1.0, 6.0, ((1, 8), (2, 2)))
    block_mask = draw_block_mask(jax.random.fold_in(jax.random.fold_in(keys[6], part), 71), part)
    return dict(queries=queries, new_keys=new_keys, new_values=new_values, history_keys=history_keys, history_values=history_values, block_mask=block_mask)


NEG = -1e+30

def reference(queries, new_keys, new_values, history_keys, history_values, block_mask):
    scale = 1.0 / math.sqrt(HD)
    group = QH // KVH
    positions = jnp.arange(NEW, dtype=jnp.int32)
    causal = positions[None, :] <= positions[:, None]

    def one_session(operands):
        query_rows, keys_new, values_new, keys_old, values_old, mask_rows = operands
        live = jnp.repeat(jnp.repeat(mask_rows, BLK, axis=0), BLK, axis=1) > 0
        visible = jnp.concatenate([live, causal], axis=1)
        keys_all = jnp.concatenate([keys_old, keys_new], axis=0).astype(jnp.float32)
        values_all = jnp.concatenate([values_old, values_new], axis=0).astype(jnp.float32)
        grouped = jnp.moveaxis(query_rows.reshape(NEW, KVH, group, HD), 1, 0).astype(jnp.float32)

        def one_head(head_ops):
            q_head, k_head, v_head = head_ops
            scores = jnp.einsum('rgd,cd->grc', q_head, k_head, precision=lax.Precision.HIGHEST) * scale
            masked = jnp.where(visible[None], scores, NEG)
            peak = lax.optimization_barrier(jnp.max(masked, axis=-1, keepdims=True))
            expo = jnp.where(visible[None], jnp.exp(masked - peak), 0.0)
            numer = jnp.einsum('grc,cd->grd', expo, v_head, precision=lax.Precision.HIGHEST)
            return numer / lax.optimization_barrier(jnp.sum(expo, axis=-1))[..., None]
        heads = lax.map(one_head, (grouped, jnp.moveaxis(keys_all, 1, 0), jnp.moveaxis(values_all, 1, 0)))
        return jnp.transpose(heads, (2, 0, 1, 3)).reshape(NEW, QH, HD)
    result = lax.map(one_session, (queries, new_keys, new_values, history_keys, history_values, block_mask))
    return result.astype(jnp.bfloat16)
```

```python
import functools
import math

import jax
import jax.numpy as jnp
from jax import lax
from jax.experimental import pallas as pl
from jax.experimental.pallas import tpu as pltpu
from jax.sharding import PartitionSpec as P

BLK = 128
NEG = -1e30
TINY = 1e-30
TOP = 32767.0
F32 = jnp.float32
BF16 = jnp.bfloat16
I16 = jnp.int16


def scores_of(q, k):
    return lax.dot_general(q, k, (((1,), (1,)), ((), ())), preferred_element_type=F32)


def xor(a, b, size):
    total, bit = 0, 1
    while bit < size:
        total = total + bit * ((a // bit + b // bit) % 2)
        bit *= 2
    return total


def remote(src, dst, send, recv, where):
    return pltpu.make_async_remote_copy(
        src_ref=src,
        dst_ref=dst,
        send_sem=send,
        recv_sem=recv,
        device_id={"ctx": where},
        device_id_type=pl.DeviceIdType.MESH,
    )


def compact(x, eye):
    return jnp.sum(jnp.where(eye, x, 0.0), axis=0, keepdims=True)


def fused_kernel(
    n, kv, own, mask_ref, q_ref, k_ref, v_ref, kn_ref, vn_ref, out_ref,
    allq_ref, kraw_ref, vraw_ref, nk_ref, nv_ref, bias_ref, kk_ref, wv_ref, kkn_ref, wvn_ref,
    s_ref, sn_ref, p_ref, pn_ref, acc_ref, den_ref, peak_ref,
    part_ref, part_st, pair_ref, pair_st, far_ref, far_st, mine_ref, got_ref,
    send_q, recv_q, send_r, recv_r, send_y, recv_y, send_k, recv_k, send_n, recv_n,
    send_p, recv_p, send_f, recv_f, send_o, recv_o,
):
    far, half = n // 2, kv // 2
    me = lax.axis_index("ctx")
    z, y = me // 2, me % 2
    partner = z * 2 + 1 - y
    rows, hd = q_ref.shape[1:]
    context = k_ref.shape[0]
    blocks = context // BLK
    both = 2 * rows
    span = min(256, both)
    group = rows // own
    factor = math.log2(math.e) / math.sqrt(hd)
    eye = lax.broadcasted_iota(jnp.int32, (128, 128), 0) == lax.broadcasted_iota(
        jnp.int32, (128, 128), 1
    )
    direct = ([1] if far > 1 else []) + list(range(2, far, 2))

    def plane(d):
        return xor(z, d, far)

    def device(d):
        return plane(d) * 2 + y

    def part_of(which):
        return pl.ds(pl.multiple_of(which * rows, rows), rows)

    def lanes_of(head, count):
        return pl.ds(pl.multiple_of(head * hd, hd), count * hd)

    barrier = pltpu.get_barrier_semaphore()
    for where in [device(d) for d in direct] + [partner]:
        pl.semaphore_signal(
            barrier, inc=1, device_id={"ctx": where}, device_id_type=pl.DeviceIdType.MESH
        )
    for t in range(2):
        for b in range(blocks):
            bias_ref[0, t, b : b + 1, :] = jnp.full(
                (1, 128), jnp.where(mask_ref[t, b] > 0, 0.0, NEG), F32
            )
    pl.semaphore_wait(barrier, len(direct) + 1)

    def swap_q(i):
        return remote(
            q_ref.at[(1 - y) * half + i], allq_ref.at[z, i, part_of(y)], send_y.at[i], recv_y.at[i], partner
        )

    def got_q(i):
        return remote(
            q_ref.at[i], allq_ref.at[z, i, part_of(1 - y)], send_y.at[i], recv_y.at[i], partner
        )

    def mine_to(i, d):
        return remote(
            q_ref.at[y * half + i], allq_ref.at[z, i, part_of(y)], send_q.at[i, d, 0], recv_q.at[i, d, 0], device(d)
        )

    def theirs_to(i, d):
        src = allq_ref.at[z, i, part_of(1 - y)]
        return remote(src, src, send_q.at[i, d, 1], recv_q.at[i, d, 1], device(d))

    def plane_from(i, d):
        return [
            remote(
                q_ref.at[i], allq_ref.at[plane(d), i, part_of(which)],
                send_q.at[i, d, at], recv_q.at[i, d, at], device(d),
            )
            for at, which in ((0, y), (1, 1 - y))
        ]

    def relay(i, d):
        src = allq_ref.at[plane(d), i]
        return remote(src, src, send_r.at[i, d], recv_r.at[i, d], device(1))

    def relayed(i, d):
        src = allq_ref.at[plane(d), i]
        return remote(src, src, send_r.at[i, d - 1], recv_r.at[i, d - 1], device(1))

    def swap_kv(i):
        lanes = lanes_of((1 - y) * half + i, 1)
        return [
            remote(k_ref.at[:, lanes], kraw_ref.at[i], send_k.at[i, 0], recv_k.at[i, 0], partner),
            remote(v_ref.at[:, lanes], vraw_ref.at[i], send_k.at[i, 1], recv_k.at[i, 1], partner),
        ]

    lanes = lanes_of((1 - y) * half, half)
    fresh = [
        remote(kn_ref.at[:, lanes], nk_ref, send_n.at[0], recv_n.at[0], partner),
        remote(vn_ref.at[:, lanes], nv_ref, send_n.at[1], recv_n.at[1], partner),
        remote(bias_ref.at[0], bias_ref.at[1], send_n.at[2], recv_n.at[2], partner),
    ]
    swap_q(0).start()
    for copy in fresh[:2]:
        copy.start()
    for i in range(1, half):
        swap_q(i).start()
    fresh[2].start()
    for i in range(half):
        for copy in swap_kv(i):
            copy.start()
    for i in range(half):
        for d in direct:
            mine_to(i, d).start()

    ones = jnp.ones((context, hd), BF16)
    for i in range(half):
        allq_ref[z, i, part_of(y)] = q_ref[y * half + i]
        lane = lanes_of(y * half + i, 1)
        k = k_ref[:, lane]
        kk_ref[i, 0, :, :hd] = k
        kk_ref[i, 0, :, hd:] = k
        wv_ref[i, 0, :, :hd] = v_ref[:, lane]
        for side in range(2):
            wv_ref[i, side, :, hd:] = ones

    def spread(i):
        swap_done = got_q(i)
        swap_done.wait_recv()
        for d in direct:
            theirs_to(i, d).start()

    spread(0)
    for copy in fresh[:2]:
        copy.wait_recv()
    blank = jnp.zeros((BLK - 2 * own, hd), BF16)
    for i in range(half):
        lane, here = lanes_of(y * half + i, 1), slice(i * hd, (i + 1) * hd)
        for mine, theirs, at in ((kn_ref[:, lane], nk_ref[:, here], 0), (vn_ref[:, lane], nv_ref[:, here], 1)):
            first = jnp.where(y == 0, mine, theirs)
            second = jnp.where(y == 0, theirs, mine)
            tile = jnp.concatenate([first, second, blank], axis=0)
            if at == 0:
                kkn_ref[i] = jnp.concatenate([tile, tile], axis=1)
            else:
                wide = jnp.concatenate([tile, jnp.ones_like(tile)], axis=1)
                wvn_ref[i] = jnp.concatenate([wide, wide], axis=0)

    def attend(i, p, side):
        qb = p * 2 * own // BLK
        for c in range(both // span):
            at = slice(c * span, (c + 1) * span)
            slot = c % 2
            q = allq_ref[p, i, at].astype(F32) * factor
            hi = q.astype(BF16)
            q = jnp.concatenate([hi, (q - hi.astype(F32)).astype(BF16)], axis=1)
            if side == 0:
                col = lax.broadcasted_iota(jnp.int32, (span, BLK), 1)
                token = (lax.broadcasted_iota(jnp.int32, (span, BLK), 0) + c * span) // group
                seen = col <= jnp.minimum(token + (p - z) * 2 * own, 2 * own - 1)
                top = jnp.where(seen, scores_of(q, kkn_ref[i]), NEG)
                sn_ref[slot] = top
            else:
                top = peak_ref[i, p, at]
            for t in range(blocks // 2):
                s = scores_of(q, kk_ref[i, side, t * 2 * BLK : (t + 1) * 2 * BLK])
                for h in range(2):
                    b = 2 * t + h
                    part = s[:, h * BLK : (h + 1) * BLK] + bias_ref[side, qb, b : b + 1, :]
                    s_ref[slot, b] = part
                    top = jnp.maximum(top, part)
            peak = jnp.maximum(jnp.max(top, axis=1, keepdims=True), 0.5 * NEG)
            for b in range(blocks):
                w = jnp.exp2(s_ref[slot, b] - peak)
                hi = w.astype(BF16)
                here = slice(b * BLK, (b + 1) * BLK)
                p_ref[slot, :span, here] = hi
                p_ref[slot, span:, here] = (w - hi.astype(F32)).astype(BF16)
            acc = jnp.dot(p_ref[slot], wv_ref[i, side], preferred_element_type=F32)
            acc = acc[:span] + acc[span:]
            if side == 0:
                w = jnp.exp2(sn_ref[slot] - peak)
                hi = w.astype(BF16)
                pn_ref[slot, :, :BLK] = hi
                pn_ref[slot, :, BLK:] = (w - hi.astype(F32)).astype(BF16)
                acc = acc + jnp.dot(pn_ref[slot], wvn_ref[i], preferred_element_type=F32)
                num, den = acc[:, :hd], acc[:, hd:]
            else:
                old = jnp.exp2(peak_ref[i, p, at] - peak)
                num = acc[:, :hd] + acc_ref[i, p, at] * old
                den = acc[:, hd:] + den_ref[i, p, at] * old
            acc_ref[i, p, at] = num
            den_ref[i, p, at] = den
            peak_ref[i, p, at] = jnp.broadcast_to(peak, (span, hd))

    chunks = both // 128

    def encode(i, p, d):
        lines = []
        for c in range(chunks):
            at = slice(c * 128, (c + 1) * 128)
            num = acc_ref[i, p, at]
            big = jnp.maximum(jnp.max(jnp.abs(num), axis=1, keepdims=True), TINY)
            part_ref[i, d, at] = jnp.floor(num * (TOP / big) + 0.5).astype(jnp.int32).astype(I16)
            lines += [
                compact(peak_ref[i, p, at], eye),
                compact(den_ref[i, p, at], eye),
                compact(jnp.broadcast_to(big * (1.0 / TOP), (128, 128)), eye),
            ]
        short = part_st.shape[2] - len(lines)
        part_st[i, d] = jnp.concatenate(lines + [jnp.zeros((short, 128), F32)], axis=0)

    def absorb(i, p, codes, stats):
        for c in range(chunks):
            at = slice(c * 128, (c + 1) * 128)
            table = jnp.concatenate([stats[3 * c : 3 * c + 3], jnp.zeros((5, 128), F32)], axis=0)
            cols = jnp.transpose(table)
            mine, theirs = peak_ref[i, p, at], cols[:, 0:1]
            peak = jnp.maximum(mine, theirs)
            old, new = jnp.exp2(mine - peak), jnp.exp2(theirs - peak)
            coded = codes[at].astype(jnp.int32).astype(F32)
            acc_ref[i, p, at] = acc_ref[i, p, at] * old + coded * (cols[:, 2:3] * new)
            den_ref[i, p, at] = den_ref[i, p, at] * old + cols[:, 1:2] * new
            peak_ref[i, p, at] = peak

    def to_pair(i, d):
        e = d // 2
        return [
            remote(part_st.at[i, d], pair_st.at[i, e], send_p.at[i, e, 0], recv_p.at[i, e, 0], device(1)),
            remote(part_ref.at[i, d], pair_ref.at[i, e], send_p.at[i, e, 1], recv_p.at[i, e, 1], device(1)),
        ]

    def to_far(i, d):
        e = d // 2
        return [
            remote(part_st.at[i, d], far_st.at[i, e], send_f.at[i, e, 0], recv_f.at[i, e, 0], device(d)),
            remote(part_ref.at[i, d], far_ref.at[i, e], send_f.at[i, e, 1], recv_f.at[i, e, 1], device(d)),
        ]

    def to_out(i):
        return remote(mine_ref.at[i], got_ref.at[i], send_o.at[i], recv_o.at[i], partner)

    def first(i, lo, hi):
        @pl.loop(lo, hi)
        def _(d):
            straight = jnp.logical_or(d % 2 == 0, d == 1)

            @pl.when(straight)
            def _():
                for copy in plane_from(i, d):
                    copy.wait_recv()

            @pl.when(d % 2 == 0)
            def _():
                relay(i, d).start()

            @pl.when(jnp.logical_not(straight))
            def _():
                relayed(i, d).wait_recv()

            attend(i, plane(d), 0)

    def odd(i):
        @pl.loop(0, far // 2)
        def _(t):
            d = far - 1 - 2 * t
            attend(i, plane(d), 1)
            encode(i, plane(d), d)
            for copy in to_pair(i, d):
                copy.start()

    def even(i):
        @pl.loop(0, far // 2 - 1)
        def _(t):
            d = far - 2 - 2 * t
            attend(i, plane(d), 1)
            for copy in to_pair(i, d):
                copy.wait_recv()
            absorb(i, plane(d), pair_ref.at[i, d // 2], pair_st.at[i, d // 2])
            encode(i, plane(d), d)
            for copy in to_far(i, d):
                copy.start()

    def finish(i):
        if far > 1:
            for copy in to_pair(i, 0):
                copy.wait_recv()
            absorb(i, z, pair_ref.at[i, 0], pair_st.at[i, 0])
        for d in range(2, far, 2):
            for copy in to_far(i, d):
                copy.wait_recv()
            absorb(i, z, far_ref.at[i, d // 2], far_st.at[i, d // 2])
        here = part_of(1 - y)
        mine_ref[i] = (acc_ref[i, z, here] / den_ref[i, z, here]).astype(BF16)
        to_out(i).start()
        here = part_of(y)
        out_ref[y * half + i] = (acc_ref[i, z, here] / den_ref[i, z, here]).astype(BF16)

    def widen(i):
        for copy in swap_kv(i):
            copy.wait_recv()
        kk_ref[i, 1, :, :hd] = kraw_ref[i]
        kk_ref[i, 1, :, hd:] = kraw_ref[i]
        wv_ref[i, 1, :, :hd] = vraw_ref[i]

    attend(0, z, 0)
    for i in range(1, half):
        spread(i)
    first(0, 1, far)
    fresh[2].wait_recv()
    for i in range(half):
        widen(i)
        if i + 1 == half and i > 0:
            odd(i)
            attend(i, z, 1)
            finish(i - 1)
            even(i)
            finish(i)
        else:
            odd(i)
            attend(i, z, 1)
            if i > 0:
                finish(i - 1)
            if i + 1 < half:
                attend(i + 1, z, 0)
                first(i + 1, 1, far)
            even(i)
            if half == 1:
                finish(i)
    for i in range(half):
        to_out(i).wait_recv()
        out_ref[(1 - y) * half + i] = got_ref[i]

    for copy in fresh:
        copy.wait_send()
    for i in range(half):
        swap_q(i).wait_send()
        to_out(i).wait_send()
        for copy in swap_kv(i):
            copy.wait_send()
        for d in direct:
            mine_to(i, d).wait_send()
            theirs_to(i, d).wait_send()
        for d in range(2, far, 2):
            relay(i, d).wait_send()
            for copy in to_far(i, d):
                copy.wait_send()
        for d in range(1, far, 2):
            for copy in to_pair(i, d):
                copy.wait_send()


def per_device(queries, new_keys, new_values, history_keys, history_values, block_mask):
    _, own, heads, hd = queries.shape
    kv = new_keys.shape[2]
    group = heads // kv
    rows = own * group
    context = history_keys.shape[1]
    blocks = context // BLK
    n = lax.axis_size("ctx")
    far, half = n // 2, kv // 2
    both = 2 * rows
    span = min(256, both)
    lines = -(-3 * (both // 128) // 8) * 8

    q = jnp.transpose(queries.reshape(own, kv, group, hd), (1, 0, 2, 3)).reshape(kv, rows, hd)
    vmem = pl.BlockSpec(memory_space=pltpu.VMEM)
    dma = pltpu.SemaphoreType.DMA
    slots = [
        pltpu.VMEM((half, far // 2, both, hd), I16),
        pltpu.VMEM((half, far // 2, lines, 128), F32),
    ]
    out = pl.pallas_call(
        functools.partial(fused_kernel, n, kv, own),
        in_specs=[pl.BlockSpec(memory_space=pltpu.SMEM)] + [vmem] * 5,
        out_specs=vmem,
        out_shape=jax.ShapeDtypeStruct((kv, rows, hd), BF16),
        scratch_shapes=[
            pltpu.VMEM((far, half, both, hd), BF16),
            pltpu.VMEM((half, context, hd), BF16),
            pltpu.VMEM((half, context, hd), BF16),
            pltpu.VMEM((own, half * hd), BF16),
            pltpu.VMEM((own, half * hd), BF16),
            pltpu.VMEM((2, 2, blocks, 128), F32),
            pltpu.VMEM((half, 2, context, 2 * hd), BF16),
            pltpu.VMEM((half, 2, context, 2 * hd), BF16),
            pltpu.VMEM((half, BLK, 2 * hd), BF16),
            pltpu.VMEM((half, 2 * BLK, 2 * hd), BF16),
            pltpu.VMEM((2, blocks, span, BLK), F32),
            pltpu.VMEM((2, span, BLK), F32),
            pltpu.VMEM((2, 2 * span, context), BF16),
            pltpu.VMEM((2, span, 2 * BLK), BF16),
            pltpu.VMEM((half, far, both, hd), F32),
            pltpu.VMEM((half, far, both, hd), F32),
            pltpu.VMEM((half, far, both, hd), F32),
            pltpu.VMEM((half, far, both, hd), I16),
            pltpu.VMEM((half, far, lines, 128), F32),
        ]
        + slots * 2
        + [
            pltpu.VMEM((half, rows, hd), BF16),
            pltpu.VMEM((half, rows, hd), BF16),
        ]
        + [dma((half, far, 2))] * 2
        + [dma((half, far))] * 2
        + [dma((half,))] * 2
        + [dma((half, 2))] * 2
        + [dma((3,))] * 2
        + [dma((half, far // 2, 2))] * 4
        + [dma((half,))] * 2,
        compiler_params=pltpu.CompilerParams(collective_id=0, has_side_effects=True),
        name="fused",
    )(
        block_mask[0],
        q,
        history_keys.reshape(context, kv * hd),
        history_values.reshape(context, kv * hd),
        new_keys.reshape(own, kv * hd),
        new_values.reshape(own, kv * hd),
    )
    out = jnp.transpose(out.reshape(kv, own, group, hd), (1, 0, 2, 3))
    return out.reshape(1, own, heads, hd)


def solution(mesh):
    spec = P("groups", "ctx", "head", None)
    return jax.shard_map(
        per_device,
        mesh=mesh,
        in_specs=(spec,) * 5 + (P("groups", None, "ctx"),),
        out_specs=spec,
        check_vma=False,
    )
```

```python
import functools
import math

import jax
import jax.numpy as jnp
from jax import lax
from jax.experimental import pallas as pl
from jax.experimental.pallas import tpu as pltpu
from jax.sharding import PartitionSpec as P

BLK = 128
NEG = -1e30
TINY = 1e-30
TOP = 32767.0
F32 = jnp.float32
BF16 = jnp.bfloat16
I16 = jnp.int16


def scores_of(q, k):
    return lax.dot_general(q, k, (((1,), (1,)), ((), ())), preferred_element_type=F32)


def xor(a, b, size):
    total, bit = 0, 1
    while bit < size:
        total = total + bit * ((a // bit + b // bit) % 2)
        bit *= 2
    return total


def remote(src, dst, send, recv, where):
    return pltpu.make_async_remote_copy(
        src_ref=src,
        dst_ref=dst,
        send_sem=send,
        recv_sem=recv,
        device_id={"ctx": where},
        device_id_type=pl.DeviceIdType.MESH,
    )


def compact(x, eye):
    return jnp.sum(jnp.where(eye, x, 0.0), axis=0, keepdims=True)


def fused_kernel(
    n, kv, own, mask_ref, q_ref, k_ref, v_ref, kn_ref, vn_ref, out_ref,
    kd_ref, vd_ref, nd_ref, allq_ref, kraw_ref, vraw_ref, nk_ref, nv_ref, bias_ref, kk_ref, wv_ref, kkn_ref, wvn_ref,
    s_ref, sn_ref, p_ref, pn_ref, acc_ref, den_ref, peak_ref,
    part_ref, part_st, pair_ref, pair_st, far_ref, far_st, mine_ref, got_ref,
    send_q, recv_q, send_r, recv_r, send_y, recv_y, send_k, recv_k, send_n, recv_n,
    send_p, recv_p, send_f, recv_f, send_o, recv_o,
):
    far, half = n // 2, kv // 2
    me = lax.axis_index("ctx")
    z, y = me // 2, me % 2
    partner = z * 2 + 1 - y
    rows, hd = q_ref.shape[1:]
    context = kraw_ref.shape[1]
    blocks = context // BLK
    both = 2 * rows
    span = min(256, both)
    group = rows // own
    factor = math.log2(math.e) / math.sqrt(hd)
    eye = lax.broadcasted_iota(jnp.int32, (128, 128), 0) == lax.broadcasted_iota(
        jnp.int32, (128, 128), 1
    )
    direct = ([1] if far > 1 else []) + list(range(2, far, 2))

    def plane(d):
        return xor(z, d, far)

    def device(d):
        return plane(d) * 2 + y

    def part_of(which):
        return pl.ds(pl.multiple_of(which * rows, rows), rows)

    barrier = pltpu.get_barrier_semaphore()
    for where in [device(d) for d in direct] + [partner]:
        pl.semaphore_signal(
            barrier, inc=1, device_id={"ctx": where}, device_id_type=pl.DeviceIdType.MESH
        )
    for t in range(2):
        for b in range(blocks):
            bias_ref[0, t, b : b + 1, :] = jnp.full(
                (1, 128), jnp.where(mask_ref[t, b] > 0, 0.0, NEG), F32
            )
    pl.semaphore_wait(barrier, len(direct) + 1)

    def swap_q(i):
        return remote(
            q_ref.at[(1 - y) * half + i], allq_ref.at[z, i, part_of(y)], send_y.at[i], recv_y.at[i], partner
        )

    def got_q(i):
        return remote(
            q_ref.at[i], allq_ref.at[z, i, part_of(1 - y)], send_y.at[i], recv_y.at[i], partner
        )

    def mine_to(i, d):
        return remote(
            q_ref.at[y * half + i], allq_ref.at[z, i, part_of(y)], send_q.at[i, d, 0], recv_q.at[i, d, 0], device(d)
        )

    def theirs_to(i, d):
        src = allq_ref.at[z, i, part_of(1 - y)]
        return remote(src, src, send_q.at[i, d, 1], recv_q.at[i, d, 1], device(d))

    def plane_from(i, d):
        return [
            remote(
                q_ref.at[i], allq_ref.at[plane(d), i, part_of(which)],
                send_q.at[i, d, at], recv_q.at[i, d, at], device(d),
            )
            for at, which in ((0, y), (1, 1 - y))
        ]

    def relay(i, d):
        src = allq_ref.at[plane(d), i]
        return remote(src, src, send_r.at[i, d], recv_r.at[i, d], device(1))

    def relayed(i, d):
        src = allq_ref.at[plane(d), i]
        return remote(src, src, send_r.at[i, d - 1], recv_r.at[i, d - 1], device(1))

    def swap_kv(i):
        head = (1 - y) * half + i
        return [
            remote(kd_ref.at[head], kraw_ref.at[i], send_k.at[i, 0], recv_k.at[i, 0], partner),
            remote(vd_ref.at[head], vraw_ref.at[i], send_k.at[i, 1], recv_k.at[i, 1], partner),
        ]

    def sorter(size):
        to = lax.broadcasted_iota(jnp.int32, (size, size), 0)
        at = lax.broadcasted_iota(jnp.int32, (size, size), 1)
        per = size // kv
        return jnp.where(at == (to % per) * kv + to // per, 1.0, 0.0).astype(BF16)

    def sort_heads(src, dst, order):
        size = order.shape[0]
        per = size // kv
        for t in range(src.shape[0] // size):
            got = jnp.dot(order, src[t * size : (t + 1) * size], preferred_element_type=F32).astype(BF16)
            for h in range(kv):
                dst[h, t * per : (t + 1) * per] = got[h * per : (h + 1) * per]

    theirs = pl.ds((1 - y) * half, half)
    fresh = [
        remote(nd_ref.at[0, theirs], nk_ref, send_n.at[0], recv_n.at[0], partner),
        remote(nd_ref.at[1, theirs], nv_ref, send_n.at[1], recv_n.at[1], partner),
        remote(bias_ref.at[0], bias_ref.at[1], send_n.at[2], recv_n.at[2], partner),
    ]
    for i in range(half):
        swap_q(i).start()
        for d in direct:
            mine_to(i, d).start()
    order = sorter(2 * BLK)
    sort_heads(k_ref, kd_ref, order)
    swap_kv(0)[0].start()
    sort_heads(v_ref, vd_ref, order)
    order = sorter(kn_ref.shape[0])
    sort_heads(kn_ref, nd_ref.at[0], order)
    sort_heads(vn_ref, nd_ref.at[1], order)
    for copy in fresh:
        copy.start()
    swap_kv(0)[1].start()
    for i in range(1, half):
        for copy in swap_kv(i):
            copy.start()

    ones = jnp.ones((context, hd), BF16)
    for i in range(half):
        allq_ref[z, i, part_of(y)] = q_ref[y * half + i]
        k = kd_ref[y * half + i]
        kk_ref[i, 0, :, :hd] = k
        kk_ref[i, 0, :, hd:] = k
        wv_ref[i, 0, :, :hd] = vd_ref[y * half + i]
        for side in range(2):
            wv_ref[i, side, :, hd:] = ones

    def spread(i):
        swap_done = got_q(i)
        swap_done.wait_recv()
        for d in direct:
            theirs_to(i, d).start()

    spread(0)
    for copy in fresh[:2]:
        copy.wait_recv()
    blank = jnp.zeros((BLK - 2 * own, hd), BF16)
    for i in range(half):
        for at, got in ((0, nk_ref[i]), (1, nv_ref[i])):
            mine = nd_ref[at, y * half + i]
            first = jnp.where(y == 0, mine, got)
            second = jnp.where(y == 0, got, mine)
            tile = jnp.concatenate([first, second, blank], axis=0)
            if at == 0:
                kkn_ref[i] = jnp.concatenate([tile, tile], axis=1)
            else:
                wide = jnp.concatenate([tile, jnp.ones_like(tile)], axis=1)
                wvn_ref[i] = jnp.concatenate([wide, wide], axis=0)

    def attend(i, p, side):
        qb = p * 2 * own // BLK
        for c in range(both // span):
            at = slice(c * span, (c + 1) * span)
            slot = c % 2
            q = allq_ref[p, i, at].astype(F32) * factor
            hi = q.astype(BF16)
            q = jnp.concatenate([hi, (q - hi.astype(F32)).astype(BF16)], axis=1)
            if side == 0:
                col = lax.broadcasted_iota(jnp.int32, (span, BLK), 1)
                token = (lax.broadcasted_iota(jnp.int32, (span, BLK), 0) + c * span) // group
                seen = col <= jnp.minimum(token + (p - z) * 2 * own, 2 * own - 1)
                top = jnp.where(seen, scores_of(q, kkn_ref[i]), NEG)
                sn_ref[slot] = top
            else:
                top = peak_ref[i, p, at]
            for t in range(blocks // 2):
                s = scores_of(q, kk_ref[i, side, t * 2 * BLK : (t + 1) * 2 * BLK])
                for h in range(2):
                    b = 2 * t + h
                    part = s[:, h * BLK : (h + 1) * BLK] + bias_ref[side, qb, b : b + 1, :]
                    s_ref[slot, b] = part
                    top = jnp.maximum(top, part)
            peak = jnp.maximum(jnp.max(top, axis=1, keepdims=True), 0.5 * NEG)
            for b in range(blocks):
                w = jnp.exp2(s_ref[slot, b] - peak)
                hi = w.astype(BF16)
                here = slice(b * BLK, (b + 1) * BLK)
                p_ref[slot, :span, here] = hi
                p_ref[slot, span:, here] = (w - hi.astype(F32)).astype(BF16)
            acc = jnp.dot(p_ref[slot], wv_ref[i, side], preferred_element_type=F32)
            acc = acc[:span] + acc[span:]
            if side == 0:
                w = jnp.exp2(sn_ref[slot] - peak)
                hi = w.astype(BF16)
                pn_ref[slot, :, :BLK] = hi
                pn_ref[slot, :, BLK:] = (w - hi.astype(F32)).astype(BF16)
                acc = acc + jnp.dot(pn_ref[slot], wvn_ref[i], preferred_element_type=F32)
                num, den = acc[:, :hd], acc[:, hd:]
            else:
                old = jnp.exp2(peak_ref[i, p, at] - peak)
                num = acc[:, :hd] + acc_ref[i, p, at] * old
                den = acc[:, hd:] + den_ref[i, p, at] * old
            acc_ref[i, p, at] = num
            den_ref[i, p, at] = den
            peak_ref[i, p, at] = jnp.broadcast_to(peak, (span, hd))

    chunks = both // 128

    def encode(i, p, d):
        lines = []
        for c in range(chunks):
            at = slice(c * 128, (c + 1) * 128)
            num = acc_ref[i, p, at]
            big = jnp.maximum(jnp.max(jnp.abs(num), axis=1, keepdims=True), TINY)
            part_ref[i, d, at] = jnp.floor(num * (TOP / big) + 0.5).astype(jnp.int32).astype(I16)
            lines += [
                compact(peak_ref[i, p, at], eye),
                compact(den_ref[i, p, at], eye),
                compact(jnp.broadcast_to(big * (1.0 / TOP), (128, 128)), eye),
            ]
        short = part_st.shape[2] - len(lines)
        part_st[i, d] = jnp.concatenate(lines + [jnp.zeros((short, 128), F32)], axis=0)

    def absorb(i, p, codes, stats):
        for c in range(chunks):
            at = slice(c * 128, (c + 1) * 128)
            table = jnp.concatenate([stats[3 * c : 3 * c + 3], jnp.zeros((5, 128), F32)], axis=0)
            cols = jnp.transpose(table)
            mine, theirs = peak_ref[i, p, at], cols[:, 0:1]
            peak = jnp.maximum(mine, theirs)
            old, new = jnp.exp2(mine - peak), jnp.exp2(theirs - peak)
            coded = codes[at].astype(jnp.int32).astype(F32)
            acc_ref[i, p, at] = acc_ref[i, p, at] * old + coded * (cols[:, 2:3] * new)
            den_ref[i, p, at] = den_ref[i, p, at] * old + cols[:, 1:2] * new
            peak_ref[i, p, at] = peak

    def to_pair(i, d):
        e = d // 2
        return [
            remote(part_st.at[i, d], pair_st.at[i, e], send_p.at[i, e, 0], recv_p.at[i, e, 0], device(1)),
            remote(part_ref.at[i, d], pair_ref.at[i, e], send_p.at[i, e, 1], recv_p.at[i, e, 1], device(1)),
        ]

    def to_far(i, d):
        e = d // 2
        return [
            remote(part_st.at[i, d], far_st.at[i, e], send_f.at[i, e, 0], recv_f.at[i, e, 0], device(d)),
            remote(part_ref.at[i, d], far_ref.at[i, e], send_f.at[i, e, 1], recv_f.at[i, e, 1], device(d)),
        ]

    def to_out(i):
        return remote(mine_ref.at[i], got_ref.at[i], send_o.at[i], recv_o.at[i], partner)

    def first(i, lo, hi):
        @pl.loop(lo, hi)
        def _(d):
            straight = jnp.logical_or(d % 2 == 0, d == 1)

            @pl.when(straight)
            def _():
                for copy in plane_from(i, d):
                    copy.wait_recv()

            @pl.when(d % 2 == 0)
            def _():
                relay(i, d).start()

            @pl.when(jnp.logical_not(straight))
            def _():
                relayed(i, d).wait_recv()

            attend(i, plane(d), 0)

    def odd(i):
        @pl.loop(0, far // 2)
        def _(t):
            d = far - 1 - 2 * t
            attend(i, plane(d), 1)
            encode(i, plane(d), d)
            for copy in to_pair(i, d):
                copy.start()

    def even(i):
        @pl.loop(0, far // 2 - 1)
        def _(t):
            d = far - 2 - 2 * t
            attend(i, plane(d), 1)
            for copy in to_pair(i, d):
                copy.wait_recv()
            absorb(i, plane(d), pair_ref.at[i, d // 2], pair_st.at[i, d // 2])
            encode(i, plane(d), d)
            for copy in to_far(i, d):
                copy.start()

    def finish(i):
        if far > 1:
            for copy in to_pair(i, 0):
                copy.wait_recv()
            absorb(i, z, pair_ref.at[i, 0], pair_st.at[i, 0])
        for d in range(2, far, 2):
            for copy in to_far(i, d):
                copy.wait_recv()
            absorb(i, z, far_ref.at[i, d // 2], far_st.at[i, d // 2])
        here = part_of(1 - y)
        mine_ref[i] = (acc_ref[i, z, here] / den_ref[i, z, here]).astype(BF16)
        to_out(i).start()
        here = part_of(y)
        out_ref[y * half + i] = (acc_ref[i, z, here] / den_ref[i, z, here]).astype(BF16)

    def widen(i):
        for copy in swap_kv(i):
            copy.wait_recv()
        kk_ref[i, 1, :, :hd] = kraw_ref[i]
        kk_ref[i, 1, :, hd:] = kraw_ref[i]
        wv_ref[i, 1, :, :hd] = vraw_ref[i]

    attend(0, z, 0)
    for i in range(1, half):
        spread(i)
    first(0, 1, far)
    fresh[2].wait_recv()
    for i in range(half):
        widen(i)
        if i + 1 == half and i > 0:
            odd(i)
            attend(i, z, 1)
            finish(i - 1)
            even(i)
            finish(i)
        else:
            odd(i)
            attend(i, z, 1)
            if i > 0:
                finish(i - 1)
            if i + 1 < half:
                attend(i + 1, z, 0)
                first(i + 1, 1, far)
            even(i)
            if half == 1:
                finish(i)
    for i in range(half):
        to_out(i).wait_recv()
        out_ref[(1 - y) * half + i] = got_ref[i]

    for copy in fresh:
        copy.wait_send()
    for i in range(half):
        swap_q(i).wait_send()
        to_out(i).wait_send()
        for copy in swap_kv(i):
            copy.wait_send()
        for d in direct:
            mine_to(i, d).wait_send()
            theirs_to(i, d).wait_send()
        for d in range(2, far, 2):
            relay(i, d).wait_send()
            for copy in to_far(i, d):
                copy.wait_send()
        for d in range(1, far, 2):
            for copy in to_pair(i, d):
                copy.wait_send()


def per_device(queries, new_keys, new_values, history_keys, history_values, block_mask):
    _, own, heads, hd = queries.shape
    kv = new_keys.shape[2]
    group = heads // kv
    rows = own * group
    context = history_keys.shape[1]
    blocks = context // BLK
    n = lax.axis_size("ctx")
    far, half = n // 2, kv // 2
    both = 2 * rows
    span = min(256, both)
    lines = -(-3 * (both // 128) // 8) * 8

    q = jnp.transpose(queries.reshape(own, kv, group, hd), (1, 0, 2, 3)).reshape(kv, rows, hd)
    vmem = pl.BlockSpec(memory_space=pltpu.VMEM)
    dma = pltpu.SemaphoreType.DMA
    slots = [
        pltpu.VMEM((half, far // 2, both, hd), I16),
        pltpu.VMEM((half, far // 2, lines, 128), F32),
    ]
    out = pl.pallas_call(
        functools.partial(fused_kernel, n, kv, own),
        in_specs=[pl.BlockSpec(memory_space=pltpu.SMEM)] + [vmem] * 5,
        out_specs=vmem,
        out_shape=jax.ShapeDtypeStruct((kv, rows, hd), BF16),
        scratch_shapes=[
            pltpu.VMEM((kv, context, hd), BF16),
            pltpu.VMEM((kv, context, hd), BF16),
            pltpu.VMEM((2, kv, own, hd), BF16),
            pltpu.VMEM((far, half, both, hd), BF16),
            pltpu.VMEM((half, context, hd), BF16),
            pltpu.VMEM((half, context, hd), BF16),
            pltpu.VMEM((half, own, hd), BF16),
            pltpu.VMEM((half, own, hd), BF16),
            pltpu.VMEM((2, 2, blocks, 128), F32),
            pltpu.VMEM((half, 2, context, 2 * hd), BF16),
            pltpu.VMEM((half, 2, context, 2 * hd), BF16),
            pltpu.VMEM((half, BLK, 2 * hd), BF16),
            pltpu.VMEM((half, 2 * BLK, 2 * hd), BF16),
            pltpu.VMEM((2, blocks, span, BLK), F32),
            pltpu.VMEM((2, span, BLK), F32),
            pltpu.VMEM((2, 2 * span, context), BF16),
            pltpu.VMEM((2, span, 2 * BLK), BF16),
            pltpu.VMEM((half, far, both, hd), F32),
            pltpu.VMEM((half, far, both, hd), F32),
            pltpu.VMEM((half, far, both, hd), F32),
            pltpu.VMEM((half, far, both, hd), I16),
            pltpu.VMEM((half, far, lines, 128), F32),
        ]
        + slots * 2
        + [
            pltpu.VMEM((half, rows, hd), BF16),
            pltpu.VMEM((half, rows, hd), BF16),
        ]
        + [dma((half, far, 2))] * 2
        + [dma((half, far))] * 2
        + [dma((half,))] * 2
        + [dma((half, 2))] * 2
        + [dma((3,))] * 2
        + [dma((half, far // 2, 2))] * 4
        + [dma((half,))] * 2,
        compiler_params=pltpu.CompilerParams(collective_id=0, has_side_effects=True),
        name="fused",
    )(
        block_mask[0],
        q,
        history_keys.reshape(context * kv, hd),
        history_values.reshape(context * kv, hd),
        new_keys.reshape(own * kv, hd),
        new_values.reshape(own * kv, hd),
    )
    out = jnp.transpose(out.reshape(kv, own, group, hd), (1, 0, 2, 3))
    return out.reshape(1, own, heads, hd)


def solution(mesh):
    spec = P("groups", "ctx", "head", None)
    return jax.shard_map(
        per_device,
        mesh=mesh,
        in_specs=(spec,) * 5 + (P("groups", None, "ctx"),),
        out_specs=spec,
        check_vma=False,
    )
```
